256 devices in a mesh: blk: 64 (over y, z, core), pair: 4 (over x).
Axes of the slice: x: 4, y: 4, z: 8, core: 2. Of those that a mesh axis runs over, the one named last changes fastest.
Arguments:
- raw_strain: bfloat16 [4, 9216, 8192], P('pair', 'blk'), may hold values from -6 to 6
- aa_taps: bfloat16 [64], replicated, may hold values from -0.75 to 0.75
- white_taps: bfloat16 [255], replicated, may hold values from -0.375 to 0.375
- src_channels: int32 [64, 64], replicated, may hold values from 0 to 8191, as said below
- recv_lo: int32 [64, 64], P('blk'), may hold values from 0 to 63
- recv_hi: int32 [64, 64], P('blk'), may hold values from 65 to 128
Outputs:
- xcorr: float32 [64, 1024, 64, 128], P('blk', 'pair')
The draws below stay inside these ranges and needn't reach their ends.
Inputs may be any that keep to these rules, and one draw needn't show every extreme that they name: `src_channels`: row b lists 64 distinct channels: exactly 2 channels from each of 32 distinct tiles and none from the other tiles; tile of channel c is c // 128.
All inputs are finite; a program needn't handle non-finite values.
Results may differ from the reference program's by a relative error of at most 0.0052.
Values may be sent and summed in bfloat16 or wider, within the bound.
A program may use at most 128 MiB of HBM per device.

```python
import math
import jax
import jax.numpy as jnp
from jax import lax

TILE = 128
CHANNELS = 8192
NT = 64
SEGS = 4
DECIM = 8
KA = 64
KW = 255
LAGS = 1024
W = 128
SEG_T = 1152
CAP = 2
NSRC = 64


def pick_tiles(subkey):
    return jax.random.permutation(subkey, NT)[:NSRC // CAP]


def pick_offsets(subkey):
    return jax.random.permutation(subkey, TILE)[:CAP]


def draw_src_channels(key, part):
    groups = NSRC // CAP
    tile_keys = jax.random.split(jax.random.fold_in(key, 11), NT)
    chan_keys = jax.random.split(jax.random.fold_in(key, 12), NT * groups)
    tile_pick = jax.vmap(pick_tiles)(tile_keys)
    offsets = jax.vmap(pick_offsets)(chan_keys).reshape(NT, groups, CAP)
    chosen = tile_pick[:, :, None] * TILE + offsets
    return chosen.reshape(NT, NSRC).astype(jnp.int32)


def with_ends(drawn, own_key, least, high):
    longest = drawn.shape.index(max(drawn.shape))
    spots = []
    for shift in (0, 1):
        where = [jax.random.randint(jax.random.fold_in(own_key, axis), (), 0, length) for axis, length in enumerate(drawn.shape)]
        where[longest] = (where[longest] + shift) % drawn.shape[longest]
        spots.append(tuple(where))
    return drawn.at[spots[0]].set(least).at[spots[1]].set(high)


def block_levels(rng, extent, cuts, least, largest):
    loudness, own = 1.0, jax.random.fold_in(rng, 6)
    for axis_at, parts in cuts:
        draws = jnp.exp(jax.random.uniform(jax.random.fold_in(own, axis_at), (parts,), jnp.float32, least / len(cuts), largest / len(cuts)))
        loudness = loudness * jnp.repeat(draws, extent[axis_at] // parts).reshape([-1 if axis == axis_at else 1 for axis in range(len(extent))])
    return loudness


def bell_draw(rng, shape, scale, reach, pieces=(), held_as=jnp.bfloat16):
    factor_of = block_levels(rng, shape, pieces, -0.22, 0.18) if pieces else 1.0
    drawn = jax.random.normal(rng, shape, jnp.float32) * scale * factor_of
    return jnp.minimum(jnp.maximum(drawn, -reach), reach).astype(held_as)


def setup_inputs(seed: int = 0) -> dict:
    keys = jax.random.split(jax.random.key(seed), 7)
    return {
        "raw_strain": bell_draw(keys[0], (SEGS, DECIM * SEG_T, CHANNELS), 1.0, 6.0, ((0, 4), (1, 64))),
        "aa_taps": bell_draw(keys[1], (KA,), KA ** -0.5, 0.75),
        "white_taps": bell_draw(keys[2], (KW,), KW ** -0.5, 0.375),
        "src_channels": draw_src_channels(jax.random.fold_in(keys[6], 71), 0),
        "recv_lo": with_ends(jax.random.randint(keys[4], (NT, NSRC), 0, TILE // 2), jax.random.fold_in(keys[4], 1), 0, (TILE // 2) - 1).astype(jnp.int32),
        "recv_hi": with_ends(jax.random.randint(keys[5], (NT, NSRC), TILE // 2 + 1, TILE + 1), jax.random.fold_in(keys[5], 1), TILE // 2 + 1, TILE).astype(jnp.int32),
    }


def decimate(segment, aa_taps):
    half = KA // 2
    padded = jnp.pad(segment.astype(jnp.float32), ((half, half), (0, 0)))
    total = jnp.zeros((SEG_T, CHANNELS), jnp.float32)
    for index in range(KA):
        total = total + aa_taps[index].astype(jnp.float32) * padded[index:index + DECIM * SEG_T:DECIM]
    return total.astype(jnp.bfloat16)

def whiten(decimated, white_taps):
    half = KW // 2
    padded = jnp.pad(decimated.astype(jnp.float32), ((half, half), (0, 0)))
    total = jnp.zeros((SEG_T, CHANNELS), jnp.float32)
    for index in range(KW):
        total = total + white_taps[index].astype(jnp.float32) * padded[index:index + SEG_T]
    return total.astype(jnp.bfloat16)

def reference(raw_strain, aa_taps, white_taps, src_channels, recv_lo, recv_hi):
    whitened = jnp.stack([whiten(decimate(raw_strain[seg], aa_taps), white_taps) for seg in range(SEGS)], 0)
    lag_block = math.gcd(128, LAGS)
    scale = 1.0 / math.sqrt(W * SEGS)

    def one_tile(tile_index):
        receivers = lax.dynamic_slice(whitened, (jnp.int32(0), jnp.int32(0), (tile_index * TILE).astype(jnp.int32)), (SEGS, SEG_T, TILE))
        chosen = jnp.take(whitened, src_channels[tile_index], axis=2)[:, LAGS // 2:LAGS // 2 + W, :].astype(jnp.float32)

        def one_block(block_index):
            window = lax.dynamic_slice(receivers, (jnp.int32(0), (block_index * lag_block).astype(jnp.int32), jnp.int32(0)), (SEGS, W + lag_block, TILE))
            hankel = jnp.stack([window[:, shift:shift + W] for shift in range(lag_block)], 2).astype(jnp.float32)
            return jnp.einsum('stk,stjr->jkr', chosen, hankel)
        blocks = lax.map(one_block, jnp.arange(LAGS // lag_block, dtype=jnp.int32))
        summed = blocks.reshape(LAGS, NSRC, TILE)
        position = jnp.arange(TILE, dtype=jnp.int32)[None, :]
        inside = (position >= recv_lo[tile_index][:, None]) & (position < recv_hi[tile_index][:, None])
        mask = jnp.where(inside, jnp.float32(scale), jnp.float32(0.0))
        return summed * mask[None]
    return lax.map(one_tile, jnp.arange(NT, dtype=jnp.int32))
```

```python
import math

import jax
import jax.numpy as jnp
from jax import lax
from jax.experimental import pallas as pl
from jax.experimental.pallas import tpu as pltpu
from jax.sharding import PartitionSpec as P

DECIM = 8
KA = 64
LAGS = 1024
BLOCK = 128
LAG_GROUP = 64
STEP_LAGS = 8


def dot(a, b, contract=((1,), (0,))):
    return lax.dot_general(a, b, (contract, ((), ())), preferred_element_type=jnp.float32)


def decimation_matrix(aa_taps, before, rows, raw_len):
    out_rows = jnp.arange(rows)[:, None] - before
    offset = jnp.arange(raw_len)[None, :] - DECIM * out_rows + KA // 2
    hit = offset[:, :, None] == jnp.arange(KA)[None, None, :]
    picked = jnp.where(hit, aa_taps.astype(jnp.float32)[None, None, :], 0.0)
    return jnp.sum(picked, axis=2).astype(aa_taps.dtype)


def whiten_kernel(span, n_pairs, dec_ref, taps_ref, src_ref, win_ref, out_ref, white_ref):
    n_blocks = dec_ref.shape[0] // BLOCK
    tile = dec_ref.shape[1]
    toeplitz = pltpu.roll(
        jnp.broadcast_to(taps_ref[...], (BLOCK, 3 * BLOCK)), 1, 1, stride=1, stride_axis=0
    ).astype(jnp.bfloat16)
    for block in range(n_blocks):
        low = max(block - 1, 0)
        high = min(block + 2, n_blocks)
        skip = (low - block + 1) * BLOCK
        rows = (high - low) * BLOCK
        white_ref[block * BLOCK : (block + 1) * BLOCK, :] = dot(
            toeplitz[:, skip : skip + rows], dec_ref[low * BLOCK : high * BLOCK, :]
        ).astype(jnp.bfloat16)
    share = LAGS // n_pairs
    for pair in range(n_pairs):
        win_ref[pair] = white_ref[pair * share : pair * share + share + span, :]
    mine = lax.axis_index("blk")
    src = src_ref[...]
    belongs = (src // tile) == mine
    chan = src - mine * tile
    first = jnp.min(jnp.where(belongs, chan, tile), axis=1, keepdims=True)
    last = jnp.max(jnp.where(belongs, chan, -1), axis=1, keepdims=True)
    lane = lax.broadcasted_iota(jnp.int32, (src.shape[0], tile), 1)
    source_time = white_ref[LAGS // 2 : LAGS // 2 + span, :]
    for slot, channel in enumerate((first, last)):
        picker = jnp.where(lane == channel, 1.0, 0.0).astype(jnp.bfloat16)
        out_ref[slot] = dot(picker, source_time, ((1,), (1,))).astype(jnp.bfloat16)


def correlate_kernel(span, n_src, got_ref, low_ref, high_ref, out_ref, lhs_ref, rhs_ref, src_ref):
    step = pl.program_id(0)
    segments, _, tile = got_ref.shape
    groups = out_ref.shape[0]
    reach = span + LAG_GROUP
    window = groups * LAG_GROUP + span

    @pl.when(step == 0)
    def _():
        gap = jnp.zeros((n_src, LAG_GROUP), jnp.float32)
        pieces = []
        for seg in range(segments):
            pieces += [got_ref[seg, window : window + n_src, :].astype(jnp.float32), gap]
            for group in range(groups):
                rhs_ref[seg * reach : (seg + 1) * reach, group * tile : (group + 1) * tile] = got_ref[
                    seg, group * LAG_GROUP : group * LAG_GROUP + reach, :
                ]
        src_ref[...] = jnp.concatenate(pieces, axis=1)

    base = src_ref[...]
    for lag in range(STEP_LAGS):
        rolled = pltpu.roll(base, lag, 1) if lag else base
        lhs_ref[lag * n_src : (lag + 1) * n_src, :] = rolled.astype(jnp.bfloat16)
    src_ref[...] = pltpu.roll(base, STEP_LAGS, 1)
    scale = 1.0 / math.sqrt(span * segments)
    position = lax.broadcasted_iota(jnp.int32, (n_src, tile), 1)
    inside = (position >= low_ref[...]) & (position < high_ref[...])
    mask = jnp.where(inside, jnp.float32(scale), jnp.float32(0.0))
    for group in range(0, groups, 2):
        product = dot(lhs_ref[...], rhs_ref[:, group * tile : (group + 2) * tile])
        for half in range(2):
            piece = product[:, half * tile : (half + 1) * tile].reshape(STEP_LAGS, n_src, tile)
            out_ref[group + half] = jnp.where(inside[None], piece * mask[None], 0.0)


def body(raw_strain, aa_taps, white_taps, src_channels, recv_lo, recv_hi):
    raw_len = raw_strain.shape[1]
    short_len = raw_len // DECIM
    channels = raw_strain.shape[2]
    n_blocks = lax.axis_size("blk")
    n_pairs = lax.axis_size("pair")
    tile = channels // n_blocks
    seg_len = short_len * n_blocks
    span = seg_len - LAGS
    n_src = src_channels.shape[1]
    n_tiles = src_channels.shape[0]
    share = LAGS // n_pairs

    before = KA // 2 // DECIM - 1
    after = KA // 2 // DECIM
    matrix = decimation_matrix(aa_taps, before, before + short_len + after, raw_len)
    partial = dot(matrix, raw_strain[0])
    ends = n_blocks - 1
    from_next = lax.ppermute(partial[:before], "blk", [(i + 1, i) for i in range(ends)])
    from_last = lax.ppermute(partial[before + short_len :], "blk", [(i, i + 1) for i in range(ends)])
    own = partial[before : before + short_len]
    decimated = jnp.concatenate(
        [
            own[:after] + from_last,
            own[after : short_len - before],
            own[short_len - before :] + from_next,
        ],
        axis=0,
    ).astype(jnp.bfloat16)
    tile_dec = lax.all_to_all(decimated, "blk", split_axis=1, concat_axis=0, tiled=True)

    taps = jnp.pad(white_taps.astype(jnp.float32), (0, 3 * BLOCK - white_taps.shape[0]))[None]
    windows, outgoing = pl.pallas_call(
        lambda *refs: whiten_kernel(span, n_pairs, *refs),
        out_shape=(
            jax.ShapeDtypeStruct((n_pairs, share + span, tile), jnp.bfloat16),
            jax.ShapeDtypeStruct((2, n_tiles, span), jnp.bfloat16),
        ),
        scratch_shapes=[pltpu.VMEM((seg_len, tile), jnp.bfloat16)],
        name="whiten",
    )(tile_dec, taps, src_channels)
    incoming = lax.all_to_all(outgoing, "blk", split_axis=1, concat_axis=1, tiled=True)
    own_src = lax.dynamic_index_in_dim(src_channels, lax.axis_index("blk"), 0, keepdims=False)
    own_tile = own_src // tile
    is_last = jnp.any(
        (own_tile[:, None] == own_tile[None, :]) & (own_src[None, :] < own_src[:, None]), axis=1
    )
    place = own_tile + jnp.where(is_last, n_tiles, 0)
    selector = (place[:, None] == jnp.arange(2 * n_tiles)[None, :]).astype(jnp.bfloat16)
    sources = dot(selector, incoming.reshape(2 * n_tiles, span)).astype(jnp.bfloat16)
    parcel = jnp.concatenate(
        [windows, jnp.broadcast_to(sources[None], (n_pairs, n_src, span))], axis=1
    )
    got = lax.all_to_all(parcel, "pair", split_axis=0, concat_axis=0, tiled=True)

    groups = share // LAG_GROUP
    reach = n_pairs * (span + LAG_GROUP)
    whole = lambda *shape: pl.BlockSpec(shape, lambda i: (0,) * len(shape))
    xcorr = pl.pallas_call(
        lambda *refs: correlate_kernel(span, n_src, *refs),
        grid=(LAG_GROUP // STEP_LAGS,),
        in_specs=[whole(*got.shape), whole(n_src, 1), whole(n_src, 1)],
        out_specs=pl.BlockSpec((groups, STEP_LAGS, n_src, tile), lambda i: (0, i, 0, 0)),
        out_shape=jax.ShapeDtypeStruct((groups, LAG_GROUP, n_src, tile), jnp.float32),
        scratch_shapes=[
            pltpu.VMEM((STEP_LAGS * n_src, reach), jnp.bfloat16),
            pltpu.VMEM((reach, groups * tile), jnp.bfloat16),
            pltpu.VMEM((n_src, reach), jnp.float32),
        ],
        name="correlate",
    )(got, recv_lo.reshape(n_src, 1), recv_hi.reshape(n_src, 1))
    return xcorr.reshape(1, share, n_src, tile)


def solution(mesh):
    placed = (P("pair", "blk", None), P(), P(), P(), P("blk", None), P("blk", None))
    return jax.shard_map(
        body, mesh=mesh, in_specs=placed, out_specs=P("blk", "pair", None, None), check_vma=False
    )
```

```python
import math

import jax
import jax.numpy as jnp
from jax import lax
from jax.experimental import pallas as pl
from jax.experimental.pallas import tpu as pltpu
from jax.sharding import PartitionSpec as P

DECIM = 8
KA = 64
LAGS = 1024
BLOCK = 128
LAG_GROUP = 64
STEP_LAGS = 8


def dot(a, b, contract=((1,), (0,))):
    return lax.dot_general(a, b, (contract, ((), ())), preferred_element_type=jnp.float32)


def rounded(value, unit):
    return -(-value // unit) * unit


def exchange_kernel(
    n_blk, n_pair, rows, span,
    raw_ref, aa_ref, taps_ref, src_ref, out_ref,
    own_ref, to_prev, to_next, from_prev, from_next, dec_ref, recv_ref,
    white_ref, offer_ref, taken_ref, pick_ref, got_ref, expand_ref,
    edge_send, edge_recv, dec_send, dec_recv, src_send, src_recv,
    win_send, win_recv, pick_send, pick_recv,
):
    me = lax.axis_index("blk")
    seg = lax.axis_index("pair")
    slot = dec_ref.shape[1]
    tile = dec_ref.shape[2]
    raw_len = raw_ref.shape[0]
    share = LAGS // n_pair
    window = share + span
    n_src = pick_ref.shape[0]
    edge = KA // 2 // DECIM

    recv_ref[...] = jnp.zeros(recv_ref.shape, recv_ref.dtype)
    barrier = pltpu.get_barrier_semaphore()

    def greet(step, carry):
        pl.semaphore_signal(barrier, inc=1, device_id={"blk": lax.rem(me + step, n_blk)})
        return carry

    lax.fori_loop(1, n_blk, greet, 0)
    for step in range(1, n_pair):
        pl.semaphore_signal(barrier, inc=1, device_id={"pair": lax.rem(seg + step, n_pair)})

    width = aa_ref.shape[1]
    lead = 2 * edge
    octets = []
    for start in range(0, rounded(lead + max(slot, rows + edge), 8), 8):
        shift = (DECIM * (start - lead) - KA // 2) % width
        shifted = pltpu.roll(jnp.broadcast_to(aa_ref[...], (8, width)), shift, 1)
        octets.append(pltpu.roll(shifted, 0, 1, stride=DECIM, stride_axis=0))
    matrix = jnp.concatenate(octets, axis=0)[:, :raw_len].astype(jnp.bfloat16)
    chunk = 8 * tile

    def decimate(index, carry):
        cols = pl.ds(pl.multiple_of(index * chunk, chunk), chunk)
        product = dot(matrix, raw_ref[:, cols])
        own_ref[:, cols] = product[lead : lead + slot]
        to_prev[:, cols] = product[lead - edge : lead]
        to_next[:, cols] = product[lead + rows : lead + rows + edge]
        return carry

    lax.fori_loop(0, n_blk // 8, decimate, 0)
    pl.semaphore_wait(barrier, n_blk - 1 + n_pair - 1)

    up = pltpu.make_async_remote_copy(
        to_next, from_prev, edge_send.at[0], edge_recv.at[0],
        device_id={"blk": lax.rem(me + 1, n_blk)},
    )
    down = pltpu.make_async_remote_copy(
        to_prev, from_next, edge_send.at[1], edge_recv.at[1],
        device_id={"blk": lax.rem(me + n_blk - 1, n_blk)},
    )
    up.start()
    down.start()

    period = 144 // rows
    depth = period * slot
    reach = taps_ref.shape[1]
    compact = pltpu.roll(
        jnp.broadcast_to(taps_ref[...], (144, reach)), 17, 1, stride=1, stride_axis=0
    ).astype(jnp.bfloat16)
    wide = lax.broadcasted_iota(jnp.int32, (reach, 3 * depth), 1)
    tall = lax.broadcasted_iota(jnp.int32, (reach, 3 * depth), 0)
    inner = lax.rem(wide, slot)
    hit = (tall == (wide // slot) * rows + inner) & (inner < rows)
    expand_ref[...] = dot(compact, jnp.where(hit, 1.0, 0.0).astype(jnp.bfloat16)).astype(
        jnp.bfloat16
    )

    up.wait()
    down.wait()

    def finish(index, carry):
        cols = pl.ds(pl.multiple_of(index * chunk, chunk), chunk)
        own_ref[0:edge, cols] += jnp.where(me > 0, from_prev[:, cols], 0.0)
        own_ref[rows - edge : rows, cols] += jnp.where(me < n_blk - 1, from_next[:, cols], 0.0)
        block = own_ref[:, cols].astype(jnp.bfloat16)
        for part in range(8):
            dec_ref[index * 8 + part] = block[:, part * tile : (part + 1) * tile]
        return carry

    lax.fori_loop(0, n_blk // 8, finish, 0)

    def block_copy(peer, place):
        return pltpu.make_async_remote_copy(
            dec_ref.at[peer, pl.ds(0, rows)], recv_ref.at[place, pl.ds(0, rows)],
            dec_send.at[peer], dec_recv.at[place], device_id={"blk": peer},
        )

    def send_block(step, carry):
        block_copy(lax.rem(me + step, n_blk), me).start()
        return carry

    def wait_block(step, carry):
        peer = lax.rem(me + step, n_blk)
        copy = block_copy(peer, peer)
        copy.wait_send()
        copy.wait_recv()
        return carry

    lax.fori_loop(1, n_blk, send_block, 0)
    recv_ref[me] = dec_ref[me]

    src = src_ref[...]
    belongs = (src // tile) == me
    chan = src - me * tile
    first = jnp.min(jnp.where(belongs, chan, tile), axis=1, keepdims=True)
    last = jnp.max(jnp.where(belongs, chan, -1), axis=1, keepdims=True)
    lane = lax.broadcasted_iota(jnp.int32, (n_blk, tile), 1)
    pickers = [
        jnp.where(lane == channel, 1.0, 0.0).astype(jnp.bfloat16) for channel in (first, last)
    ]
    row = src_ref[pl.ds(me, 1), :]
    square = (n_src, n_src)
    across = jnp.broadcast_to(row, square).astype(jnp.float32)
    diagonal = lax.broadcasted_iota(jnp.int32, square, 0) == lax.broadcasted_iota(
        jnp.int32, square, 1
    )
    column = jnp.sum(jnp.where(diagonal, across, 0.0), axis=1, keepdims=True)
    column = column.astype(jnp.int32)
    same = (row // tile) == (column // tile)
    later = jnp.max(jnp.where(same & (row < column), 1.0, 0.0), axis=1, keepdims=True)
    owner = lax.broadcasted_iota(jnp.int32, (n_src, n_blk), 1) == (column // tile)
    selectors = [
        jnp.where(owner & (later == float(which)), 1.0, 0.0).astype(jnp.bfloat16)
        for which in range(2)
    ]

    lax.fori_loop(1, n_blk, wait_block, 0)

    groups = n_blk // period
    for group in range(groups):
        low, high = max(group - 1, 0), min(group + 2, groups)
        skip = (low - group + 1) * depth
        held = recv_ref[low * period : high * period].reshape((high - low) * depth, tile)
        white_ref[group * 144 : (group + 1) * 144, :] = dot(
            expand_ref[:, skip : skip + (high - low) * depth], held
        ).astype(jnp.bfloat16)

    source_time = white_ref[LAGS // 2 : LAGS // 2 + span, :]
    for which in range(2):
        offer_ref[:, which, :] = dot(pickers[which], source_time, ((1,), (1,)))

    def source_copy(peer, place):
        return pltpu.make_async_remote_copy(
            offer_ref.at[peer], taken_ref.at[place],
            src_send.at[peer], src_recv.at[place], device_id={"blk": peer},
        )

    def send_source(step, carry):
        source_copy(lax.rem(me + step, n_blk), me).start()
        return carry

    def wait_source(step, carry):
        peer = lax.rem(me + step, n_blk)
        copy = source_copy(peer, peer)
        copy.wait_send()
        copy.wait_recv()
        return carry

    def window_copy(peer, place):
        return pltpu.make_async_remote_copy(
            white_ref.at[pl.ds(pl.multiple_of(peer * share, share), window)],
            got_ref.at[place, pl.ds(0, window)],
            win_send.at[peer], win_recv.at[place], device_id={"pair": peer},
        )

    def pick_copy(peer, place):
        return pltpu.make_async_remote_copy(
            pick_ref, got_ref.at[place, pl.ds(window, n_src)],
            pick_send.at[peer], pick_recv.at[place], device_id={"pair": peer},
        )

    pair_peers = [lax.rem(seg + step, n_pair) for step in range(1, n_pair)]
    lax.fori_loop(1, n_blk, send_source, 0)
    for peer in pair_peers:
        window_copy(peer, seg).start()
    taken_ref[me] = offer_ref[me]
    got_ref[seg, 0:window] = white_ref[pl.ds(pl.multiple_of(seg * share, share), window), :]
    lax.fori_loop(1, n_blk, wait_source, 0)
    picked = jnp.zeros((n_src, span), jnp.float32)
    for which in range(2):
        picked += dot(selectors[which], taken_ref[:, which, :].astype(jnp.bfloat16))
    pick_ref[...] = picked.astype(jnp.bfloat16)
    for peer in pair_peers:
        pick_copy(peer, seg).start()
    got_ref[seg, window : window + n_src] = picked.astype(jnp.bfloat16)
    for peer in pair_peers:
        for copy in (window_copy(peer, peer), pick_copy(peer, peer)):
            copy.wait_send()
            copy.wait_recv()
    out_ref[...] = got_ref[...]


def correlate_kernel(span, n_src, got_ref, low_ref, high_ref, out_ref, lhs_ref, rhs_ref, src_ref):
    step = pl.program_id(0)
    segments, _, tile = got_ref.shape
    groups = out_ref.shape[0]
    reach = span + LAG_GROUP
    window = groups * LAG_GROUP + span

    @pl.when(step == 0)
    def _():
        gap = jnp.zeros((n_src, LAG_GROUP), jnp.float32)
        pieces = []
        for seg in range(segments):
            pieces += [got_ref[seg, window : window + n_src, :].astype(jnp.float32), gap]
            for group in range(groups):
                rhs_ref[seg * reach : (seg + 1) * reach, group * tile : (group + 1) * tile] = got_ref[
                    seg, group * LAG_GROUP : group * LAG_GROUP + reach, :
                ]
        src_ref[...] = jnp.concatenate(pieces, axis=1)

    base = src_ref[...]
    for lag in range(STEP_LAGS):
        rolled = pltpu.roll(base, lag, 1) if lag else base
        lhs_ref[lag * n_src : (lag + 1) * n_src, :] = rolled.astype(jnp.bfloat16)
    src_ref[...] = pltpu.roll(base, STEP_LAGS, 1)
    scale = 1.0 / math.sqrt(span * segments)
    position = lax.broadcasted_iota(jnp.int32, (n_src, tile), 1)
    inside = (position >= low_ref[...]) & (position < high_ref[...])
    mask = jnp.where(inside, jnp.float32(scale), jnp.float32(0.0))
    for group in range(0, groups, 2):
        product = dot(lhs_ref[...], rhs_ref[:, group * tile : (group + 2) * tile])
        for half in range(2):
            piece = product[:, half * tile : (half + 1) * tile].reshape(STEP_LAGS, n_src, tile)
            out_ref[group + half] = jnp.where(inside[None], piece * mask[None], 0.0)


def body(raw_strain, aa_taps, white_taps, src_channels, recv_lo, recv_hi):
    raw_len = raw_strain.shape[1]
    short_len = raw_len // DECIM
    channels = raw_strain.shape[2]
    n_blocks = lax.axis_size("blk")
    n_pairs = lax.axis_size("pair")
    tile = channels // n_blocks
    seg_len = short_len * n_blocks
    span = seg_len - LAGS
    n_src = src_channels.shape[1]
    n_tiles = src_channels.shape[0]
    share = LAGS // n_pairs

    slot = rounded(short_len, 16)
    edge = KA // 2 // DECIM
    aa_width = rounded(DECIM * (slot + 3 * edge) + KA + KA // 2, BLOCK)
    aa_row = jnp.pad(aa_taps.astype(jnp.float32), (0, aa_width - KA))[None]
    taps = jnp.pad(white_taps.astype(jnp.float32), (0, 4 * BLOCK - white_taps.shape[0]))[None]
    depth = 144 // short_len * slot
    dma = pltpu.SemaphoreType.DMA
    vmem = pl.BlockSpec(memory_space=pltpu.VMEM)
    got = pl.pallas_call(
        lambda *refs: exchange_kernel(n_blocks, n_pairs, short_len, span, *refs),
        in_specs=[vmem] * 4,
        out_specs=vmem,
        out_shape=jax.ShapeDtypeStruct((n_pairs, share + span + n_src, tile), jnp.bfloat16),
        scratch_shapes=[
            pltpu.VMEM((slot, channels), jnp.float32),
            *[pltpu.VMEM((edge, channels), jnp.float32)] * 4,
            *[pltpu.VMEM((n_blocks, slot, tile), jnp.bfloat16)] * 2,
            pltpu.VMEM((seg_len, tile), jnp.bfloat16),
            *[pltpu.VMEM((n_tiles, 2, span), jnp.float32)] * 2,
            pltpu.VMEM((n_src, span), jnp.bfloat16),
            pltpu.VMEM((n_pairs, share + span + n_src, tile), jnp.bfloat16),
            pltpu.VMEM((144, 3 * depth), jnp.bfloat16),
            dma((2,)), dma((2,)),
            *[dma((n_blocks,))] * 4,
            *[dma((n_pairs,))] * 4,
        ],
        compiler_params=pltpu.CompilerParams(collective_id=0, has_side_effects=True),
        name="exchange",
    )(raw_strain[0], aa_row, taps, src_channels)

    groups = share // LAG_GROUP
    reach = n_pairs * (span + LAG_GROUP)
    whole = lambda *shape: pl.BlockSpec(shape, lambda i: (0,) * len(shape))
    xcorr = pl.pallas_call(
        lambda *refs: correlate_kernel(span, n_src, *refs),
        grid=(LAG_GROUP // STEP_LAGS,),
        in_specs=[whole(*got.shape), whole(n_src, 1), whole(n_src, 1)],
        out_specs=pl.BlockSpec((groups, STEP_LAGS, n_src, tile), lambda i: (0, i, 0, 0)),
        out_shape=jax.ShapeDtypeStruct((groups, LAG_GROUP, n_src, tile), jnp.float32),
        scratch_shapes=[
            pltpu.VMEM((STEP_LAGS * n_src, reach), jnp.bfloat16),
            pltpu.VMEM((reach, groups * tile), jnp.bfloat16),
            pltpu.VMEM((n_src, reach), jnp.float32),
        ],
        name="correlate",
    )(got, recv_lo.reshape(n_src, 1), recv_hi.reshape(n_src, 1))
    return xcorr.reshape(1, share, n_src, tile)


def solution(mesh):
    placed = (P("pair", "blk", None), P(), P(), P(), P("blk", None), P("blk", None))
    return jax.shard_map(
        body, mesh=mesh, in_specs=placed, out_specs=P("blk", "pair", None, None), check_vma=False
    )
```

```python
import math

import jax
import jax.numpy as jnp
from jax import lax
from jax.experimental import pallas as pl
from jax.experimental.pallas import tpu as pltpu
from jax.sharding import PartitionSpec as P

DECIM = 8
KA = 64
LAGS = 1024
BLOCK = 128
LAG_GROUP = 64
STEP_LAGS = 8


def dot(a, b, contract=((1,), (0,))):
    return lax.dot_general(a, b, (contract, ((), ())), preferred_element_type=jnp.float32)


def rounded(value, unit):
    return -(-value // unit) * unit


def turned(row):
    square = (row.shape[1], row.shape[1])
    diagonal = lax.broadcasted_iota(jnp.int32, square, 0) == lax.broadcasted_iota(
        jnp.int32, square, 1
    )
    across = jnp.broadcast_to(row, square).astype(jnp.float32)
    return jnp.sum(jnp.where(diagonal, across, 0.0), axis=1, keepdims=True).astype(jnp.int32)


def exchange_kernel(
    n_blk, n_pair, rows, span,
    raw_hbm, aa_in, taps_in, src_ref, out_ref,
    raw_ref, aa_ref, taps_ref,
    own_ref, to_prev, to_next, from_prev, from_next, dec_ref, recv_ref,
    white_ref, offer_ref, taken_ref, pick_ref, got_ref, expand_ref,
    edge_send, edge_recv, dec_send, dec_recv, src_send, src_recv,
    win_send, win_recv, pick_send, pick_recv, raw_sem,
):
    me = lax.axis_index("blk")
    seg = lax.axis_index("pair")
    slot = dec_ref.shape[1]
    tile = dec_ref.shape[2]
    raw_len = raw_ref.shape[0]
    share = LAGS // n_pair
    window = share + span
    n_src = pick_ref.shape[0]
    edge = KA // 2 // DECIM

    recv_ref[...] = jnp.zeros(recv_ref.shape, recv_ref.dtype)
    barrier = pltpu.get_barrier_semaphore()

    def greet(step, carry):
        pl.semaphore_signal(barrier, inc=1, device_id={"blk": lax.rem(me + step, n_blk)})
        return carry

    lax.fori_loop(1, n_blk, greet, 0)
    for step in range(1, n_pair):
        pl.semaphore_signal(barrier, inc=1, device_id={"pair": lax.rem(seg + step, n_pair)})

    chunk = 8 * tile

    def raw_copy(index):
        cols = pl.ds(pl.multiple_of(index * chunk, chunk), chunk)
        return pltpu.make_async_copy(raw_hbm.at[:, cols], raw_ref.at[:, cols], raw_sem.at[index])

    for index in range(n_blk // 8):
        raw_copy(index).start()
    for wide_ref, given in ((aa_ref, aa_in), (taps_ref, taps_in)):
        wide_ref[...] = jnp.zeros(wide_ref.shape, wide_ref.dtype)
        wide_ref[:, : given.shape[0]] = given[...].astype(jnp.float32).reshape(1, given.shape[0])
    width = aa_ref.shape[1]
    lead = 2 * edge
    octets = []
    for start in range(0, rounded(lead + max(slot, rows + edge), 8), 8):
        shift = (DECIM * (start - lead) - KA // 2) % width
        shifted = pltpu.roll(jnp.broadcast_to(aa_ref[...], (8, width)), shift, 1)
        octets.append(pltpu.roll(shifted, 0, 1, stride=DECIM, stride_axis=0))
    matrix = jnp.concatenate(octets, axis=0)[:, :raw_len].astype(jnp.bfloat16)

    def decimate(index, carry):
        raw_copy(index).wait()
        cols = pl.ds(pl.multiple_of(index * chunk, chunk), chunk)
        product = dot(matrix, raw_ref[:, cols])
        own_ref[:, cols] = product[lead : lead + slot]
        to_prev[:, cols] = product[lead - edge : lead]
        to_next[:, cols] = product[lead + rows : lead + rows + edge]
        return carry

    lax.fori_loop(0, n_blk // 8, decimate, 0)
    pl.semaphore_wait(barrier, n_blk - 1 + n_pair - 1)

    up = pltpu.make_async_remote_copy(
        to_next, from_prev, edge_send.at[0], edge_recv.at[0],
        device_id={"blk": lax.rem(me + 1, n_blk)},
    )
    down = pltpu.make_async_remote_copy(
        to_prev, from_next, edge_send.at[1], edge_recv.at[1],
        device_id={"blk": lax.rem(me + n_blk - 1, n_blk)},
    )
    up.start()
    down.start()

    period = 144 // rows
    depth = period * slot
    reach = taps_ref.shape[1]
    compact = pltpu.roll(
        jnp.broadcast_to(taps_ref[...], (144, reach)), 17, 1, stride=1, stride_axis=0
    ).astype(jnp.bfloat16)
    wide = lax.broadcasted_iota(jnp.int32, (reach, 3 * depth), 1)
    tall = lax.broadcasted_iota(jnp.int32, (reach, 3 * depth), 0)
    inner = lax.rem(wide, slot)
    hit = (tall == (wide // slot) * rows + inner) & (inner < rows)
    expand_ref[...] = dot(compact, jnp.where(hit, 1.0, 0.0).astype(jnp.bfloat16)).astype(
        jnp.bfloat16
    )

    up.wait()
    down.wait()

    def finish(index, carry):
        cols = pl.ds(pl.multiple_of(index * chunk, chunk), chunk)
        own_ref[0:edge, cols] += jnp.where(me > 0, from_prev[:, cols], 0.0)
        own_ref[rows - edge : rows, cols] += jnp.where(me < n_blk - 1, from_next[:, cols], 0.0)
        block = own_ref[:, cols].astype(jnp.bfloat16)
        for part in range(8):
            dec_ref[index * 8 + part] = block[:, part * tile : (part + 1) * tile]
        return carry

    lax.fori_loop(0, n_blk // 8, finish, 0)

    def block_copy(peer, place):
        return pltpu.make_async_remote_copy(
            dec_ref.at[peer, pl.ds(0, rows)], recv_ref.at[place, pl.ds(0, rows)],
            dec_send.at[peer], dec_recv.at[place], device_id={"blk": peer},
        )

    def send_block(step, carry):
        block_copy(lax.rem(me + step, n_blk), me).start()
        return carry

    def wait_block(step, carry):
        peer = lax.rem(me + step, n_blk)
        copy = block_copy(peer, peer)
        copy.wait_send()
        copy.wait_recv()
        return carry

    lax.fori_loop(1, n_blk, send_block, 0)
    recv_ref[me] = dec_ref[me]

    src = src_ref[...]
    belongs = (src // tile) == me
    chan = src - me * tile
    first = jnp.min(jnp.where(belongs, chan, tile), axis=1, keepdims=True)
    last = jnp.max(jnp.where(belongs, chan, -1), axis=1, keepdims=True)
    lane = lax.broadcasted_iota(jnp.int32, (n_blk, tile), 1)
    pickers = [
        jnp.where(lane == channel, 1.0, 0.0).astype(jnp.bfloat16) for channel in (first, last)
    ]
    row = src_ref[pl.ds(me, 1), :]
    column = turned(row)
    same = (row // tile) == (column // tile)
    later = jnp.max(jnp.where(same & (row < column), 1.0, 0.0), axis=1, keepdims=True)
    owner = lax.broadcasted_iota(jnp.int32, (n_src, n_blk), 1) == (column // tile)
    selectors = [
        jnp.where(owner & (later == float(which)), 1.0, 0.0).astype(jnp.bfloat16)
        for which in range(2)
    ]

    lax.fori_loop(1, n_blk, wait_block, 0)

    groups = n_blk // period
    for group in range(groups):
        low, high = max(group - 1, 0), min(group + 2, groups)
        skip = (low - group + 1) * depth
        held = recv_ref[low * period : high * period].reshape((high - low) * depth, tile)
        white_ref[group * 144 : (group + 1) * 144, :] = dot(
            expand_ref[:, skip : skip + (high - low) * depth], held
        ).astype(jnp.bfloat16)

    source_time = white_ref[LAGS // 2 : LAGS // 2 + span, :]
    for which in range(2):
        offer_ref[:, which, :] = dot(pickers[which], source_time, ((1,), (1,)))

    def source_copy(peer, place):
        return pltpu.make_async_remote_copy(
            offer_ref.at[peer], taken_ref.at[place],
            src_send.at[peer], src_recv.at[place], device_id={"blk": peer},
        )

    def send_source(step, carry):
        source_copy(lax.rem(me + step, n_blk), me).start()
        return carry

    def wait_source(step, carry):
        peer = lax.rem(me + step, n_blk)
        copy = source_copy(peer, peer)
        copy.wait_send()
        copy.wait_recv()
        return carry

    def window_copy(peer, place):
        return pltpu.make_async_remote_copy(
            white_ref.at[pl.ds(pl.multiple_of(peer * share, share), window)],
            got_ref.at[place, pl.ds(0, window)],
            win_send.at[peer], win_recv.at[place], device_id={"pair": peer},
        )

    def pick_copy(peer, place):
        return pltpu.make_async_remote_copy(
            pick_ref, got_ref.at[place, pl.ds(window, n_src)],
            pick_send.at[peer], pick_recv.at[place], device_id={"pair": peer},
        )

    pair_peers = [lax.rem(seg + step, n_pair) for step in range(1, n_pair)]
    pair_peers = pair_peers[1:] + pair_peers[:1]
    lax.fori_loop(1, n_blk, send_source, 0)
    for peer in pair_peers:
        window_copy(peer, seg).start()
    taken_ref[me] = offer_ref[me]
    got_ref[seg, 0:window] = white_ref[pl.ds(pl.multiple_of(seg * share, share), window), :]
    lax.fori_loop(1, n_blk, wait_source, 0)
    picked = jnp.zeros((n_src, span), jnp.float32)
    for which in range(2):
        picked += dot(selectors[which], taken_ref[:, which, :].astype(jnp.bfloat16))
    pick_ref[...] = picked.astype(jnp.bfloat16)
    for peer in pair_peers:
        pick_copy(peer, seg).start()
    got_ref[seg, window : window + n_src] = picked.astype(jnp.bfloat16)
    for peer in pair_peers:
        for copy in (window_copy(peer, peer), pick_copy(peer, peer)):
            copy.wait_send()
            copy.wait_recv()
    out_ref[...] = got_ref[...]


def correlate_kernel(span, n_src, got_ref, low_ref, high_ref, out_ref, lhs_ref, rhs_ref, src_ref, mask_ref):
    step = pl.program_id(0)
    segments, _, tile = got_ref.shape
    groups = out_ref.shape[0]
    reach = span + LAG_GROUP
    window = groups * LAG_GROUP + span

    @pl.when(step == 0)
    def _():
        gap = jnp.zeros((n_src, LAG_GROUP), jnp.float32)
        pieces = []
        for seg in range(segments):
            pieces += [got_ref[seg, window : window + n_src, :].astype(jnp.float32), gap]
            for group in range(groups):
                rhs_ref[seg * reach : (seg + 1) * reach, group * tile : (group + 1) * tile] = got_ref[
                    seg, group * LAG_GROUP : group * LAG_GROUP + reach, :
                ]
        src_ref[...] = jnp.concatenate(pieces, axis=1)
        low, high = turned(low_ref[...]), turned(high_ref[...])
        position = lax.broadcasted_iota(jnp.int32, (n_src, tile), 1)
        inside = (position >= low) & (position < high)
        scale = 1.0 / math.sqrt(span * segments)
        mask_ref[...] = jnp.where(inside, jnp.float32(scale), jnp.float32(0.0))

    base = src_ref[...]
    for lag in range(STEP_LAGS):
        rolled = pltpu.roll(base, lag, 1) if lag else base
        lhs_ref[lag * n_src : (lag + 1) * n_src, :] = rolled.astype(jnp.bfloat16)
    src_ref[...] = pltpu.roll(base, STEP_LAGS, 1)
    mask = mask_ref[...]
    for group in range(0, groups, 2):
        product = dot(lhs_ref[...], rhs_ref[:, group * tile : (group + 2) * tile])
        for half in range(2):
            piece = product[:, half * tile : (half + 1) * tile].reshape(STEP_LAGS, n_src, tile)
            out_ref[group + half] = piece * mask[None]


def body(raw_strain, aa_taps, white_taps, src_channels, recv_lo, recv_hi):
    raw_len = raw_strain.shape[1]
    short_len = raw_len // DECIM
    channels = raw_strain.shape[2]
    n_blocks = lax.axis_size("blk")
    n_pairs = lax.axis_size("pair")
    tile = channels // n_blocks
    seg_len = short_len * n_blocks
    span = seg_len - LAGS
    n_src = src_channels.shape[1]
    n_tiles = src_channels.shape[0]
    share = LAGS // n_pairs

    slot = rounded(short_len, 16)
    edge = KA // 2 // DECIM
    aa_width = rounded(DECIM * (slot + 3 * edge) + KA + KA // 2, BLOCK)
    depth = 144 // short_len * slot
    dma = pltpu.SemaphoreType.DMA
    vmem = pl.BlockSpec(memory_space=pltpu.VMEM)
    got = pl.pallas_call(
        lambda *refs: exchange_kernel(n_blocks, n_pairs, short_len, span, *refs),
        in_specs=[pl.BlockSpec(memory_space=pl.ANY)] + [vmem] * 3,
        out_specs=vmem,
        out_shape=jax.ShapeDtypeStruct((n_pairs, share + span + n_src, tile), jnp.bfloat16),
        scratch_shapes=[
            pltpu.VMEM((raw_len, channels), raw_strain.dtype),
            pltpu.VMEM((1, aa_width), jnp.float32),
            pltpu.VMEM((1, 4 * BLOCK), jnp.float32),
            pltpu.VMEM((slot, channels), jnp.float32),
            *[pltpu.VMEM((edge, channels), jnp.float32)] * 4,
            *[pltpu.VMEM((n_blocks, slot, tile), jnp.bfloat16)] * 2,
            pltpu.VMEM((seg_len, tile), jnp.bfloat16),
            *[pltpu.VMEM((n_tiles, 2, span), jnp.float32)] * 2,
            pltpu.VMEM((n_src, span), jnp.bfloat16),
            pltpu.VMEM((n_pairs, share + span + n_src, tile), jnp.bfloat16),
            pltpu.VMEM((144, 3 * depth), jnp.bfloat16),
            dma((2,)), dma((2,)),
            *[dma((n_blocks,))] * 4,
            *[dma((n_pairs,))] * 4,
            dma((n_blocks // 8,)),
        ],
        compiler_params=pltpu.CompilerParams(collective_id=0, has_side_effects=True),
        name="exchange",
    )(raw_strain[0], aa_taps, white_taps, src_channels)

    groups = share // LAG_GROUP
    reach = n_pairs * (span + LAG_GROUP)
    whole = lambda *shape: pl.BlockSpec(shape, lambda i: (0,) * len(shape))
    xcorr = pl.pallas_call(
        lambda *refs: correlate_kernel(span, n_src, *refs),
        grid=(LAG_GROUP // STEP_LAGS,),
        in_specs=[whole(*got.shape), whole(1, n_src), whole(1, n_src)],
        out_specs=pl.BlockSpec((groups, STEP_LAGS, n_src, tile), lambda i: (0, i, 0, 0)),
        out_shape=jax.ShapeDtypeStruct((groups, LAG_GROUP, n_src, tile), jnp.float32),
        scratch_shapes=[
            pltpu.VMEM((STEP_LAGS * n_src, reach), jnp.bfloat16),
            pltpu.VMEM((reach, groups * tile), jnp.bfloat16),
            pltpu.VMEM((n_src, reach), jnp.float32),
            pltpu.VMEM((n_src, tile), jnp.float32),
        ],
        name="correlate",
    )(got, recv_lo, recv_hi)
    return xcorr.reshape(1, share, n_src, tile)


def solution(mesh):
    placed = (P("pair", "blk", None), P(), P(), P(), P("blk", None), P("blk", None))
    return jax.shard_map(
        body, mesh=mesh, in_specs=placed, out_specs=P("blk", "pair", None, None), check_vma=False
    )
```

```python
import math

import jax
import jax.numpy as jnp
from jax import lax
from jax.experimental import pallas as pl
from jax.experimental.pallas import tpu as pltpu
from jax.sharding import PartitionSpec as P

DECIM = 8
KA = 64
LAGS = 1024
BLOCK = 128
LAG_GROUP = 64
STEP_LAGS = 8


def dot(a, b, contract=((1,), (0,))):
    return lax.dot_general(a, b, (contract, ((), ())), preferred_element_type=jnp.float32)


def rounded(value, unit):
    return -(-value // unit) * unit


def turned(row):
    square = (row.shape[1], row.shape[1])
    diagonal = lax.broadcasted_iota(jnp.int32, square, 0) == lax.broadcasted_iota(
        jnp.int32, square, 1
    )
    across = jnp.broadcast_to(row, square).astype(jnp.float32)
    return jnp.sum(jnp.where(diagonal, across, 0.0), axis=1, keepdims=True).astype(jnp.int32)


def exchange_kernel(
    n_blk, n_pair, rows, span,
    raw_hbm, aa_in, taps_in, src_ref, out_ref,
    raw_ref, aa_ref, taps_ref,
    edges_ref, to_prev, to_next, from_prev, from_next, dec_ref, recv_ref,
    white_ref, offer_ref, taken_ref, pick_ref, got_ref, expand_ref,
    edge_send, edge_recv, dec_send, dec_recv, src_send, src_recv,
    win_send, win_recv, pick_send, pick_recv, raw_sem,
):
    me = lax.axis_index("blk")
    seg = lax.axis_index("pair")
    slot = dec_ref.shape[1]
    tile = dec_ref.shape[2]
    raw_len = raw_ref.shape[0]
    share = LAGS // n_pair
    window = share + span
    n_src = pick_ref.shape[0]
    edge = KA // 2 // DECIM
    inner = rows - 2 * edge
    inner_slot = slot - 16

    recv_ref[...] = jnp.zeros(recv_ref.shape, recv_ref.dtype)
    barrier = pltpu.get_barrier_semaphore()

    def greet(step, carry):
        pl.semaphore_signal(barrier, inc=1, device_id={"blk": lax.rem(me + step, n_blk)})
        return carry

    lax.fori_loop(1, n_blk, greet, 0)
    for step in range(1, n_pair):
        pl.semaphore_signal(barrier, inc=1, device_id={"pair": lax.rem(seg + step, n_pair)})

    chunk = 8 * tile

    def raw_copy(index):
        cols = pl.ds(pl.multiple_of(index * chunk, chunk), chunk)
        return pltpu.make_async_copy(raw_hbm.at[:, cols], raw_ref.at[:, cols], raw_sem.at[index])

    for index in range(n_blk // 8):
        raw_copy(index).start()
    for wide_ref, given in ((aa_ref, aa_in), (taps_ref, taps_in)):
        wide_ref[...] = jnp.zeros(wide_ref.shape, wide_ref.dtype)
        wide_ref[:, : given.shape[0]] = given[...].astype(jnp.float32).reshape(1, given.shape[0])
    width = aa_ref.shape[1]
    lead = 2 * edge
    octets = []
    for start in range(0, rounded(lead + slot + edge, 8), 8):
        shift = (DECIM * (start - lead) - KA // 2) % width
        shifted = pltpu.roll(jnp.broadcast_to(aa_ref[...], (8, width)), shift, 1)
        octets.append(pltpu.roll(shifted, 0, 1, stride=DECIM, stride_axis=0))
    matrix = jnp.concatenate(octets, axis=0)[:, :raw_len].astype(jnp.bfloat16)

    def decimate(index, carry):
        raw_copy(index).wait()
        cols = pl.ds(pl.multiple_of(index * chunk, chunk), chunk)
        product = dot(matrix, raw_ref[:, cols])
        edges_ref[0:edge, cols] = product[lead : lead + edge]
        edges_ref[edge : 2 * edge, cols] = product[lead + rows - edge : lead + rows]
        inside = product[lead + edge : lead + edge + inner_slot].astype(jnp.bfloat16)
        for part in range(8):
            dec_ref[index * 8 + part, 0:inner_slot] = inside[:, part * tile : (part + 1) * tile]
        to_prev[:, cols] = product[lead - edge : lead]
        to_next[:, cols] = product[lead + rows : lead + rows + edge]
        return carry

    lax.fori_loop(0, n_blk // 8, decimate, 0)
    pl.semaphore_wait(barrier, n_blk - 1 + n_pair - 1)

    up = pltpu.make_async_remote_copy(
        to_next, from_prev, edge_send.at[0], edge_recv.at[0],
        device_id={"blk": lax.rem(me + 1, n_blk)},
    )
    down = pltpu.make_async_remote_copy(
        to_prev, from_next, edge_send.at[1], edge_recv.at[1],
        device_id={"blk": lax.rem(me + n_blk - 1, n_blk)},
    )
    up.start()
    down.start()

    def block_copy(peer, place, piece):
        part = pl.ds(0, inner) if piece == 0 else pl.ds(inner_slot, 2 * edge)
        return pltpu.make_async_remote_copy(
            dec_ref.at[peer, part], recv_ref.at[place, part],
            dec_send.at[piece, peer], dec_recv.at[piece, place], device_id={"blk": peer},
        )

    def send_block(piece):
        def send(step, carry):
            block_copy(lax.rem(me + step, n_blk), me, piece).start()
            return carry

        lax.fori_loop(1, n_blk, send, 0)

    def wait_block(step, carry):
        peer = lax.rem(me + step, n_blk)
        for piece in range(2):
            copy = block_copy(peer, peer, piece)
            copy.wait_send()
            copy.wait_recv()
        return carry

    send_block(0)
    up.wait()
    down.wait()

    def finish(index, carry):
        cols = pl.ds(pl.multiple_of(index * chunk, chunk), chunk)
        head = edges_ref[0:edge, cols] + jnp.where(me > 0, from_prev[:, cols], 0.0)
        foot = edges_ref[edge : 2 * edge, cols]
        foot += jnp.where(me < n_blk - 1, from_next[:, cols], 0.0)
        block = jnp.concatenate([head, foot], axis=0).astype(jnp.bfloat16)
        for part in range(8):
            dec_ref[index * 8 + part, inner_slot : inner_slot + 2 * edge] = block[
                :, part * tile : (part + 1) * tile
            ]
        return carry

    lax.fori_loop(0, n_blk // 8, finish, 0)
    send_block(1)
    recv_ref[me, 0:inner] = dec_ref[me, 0:inner]
    recv_ref[me, inner_slot : inner_slot + 2 * edge] = dec_ref[
        me, inner_slot : inner_slot + 2 * edge
    ]

    period = 144 // rows
    depth = period * slot
    reach = taps_ref.shape[1]
    compact = pltpu.roll(
        jnp.broadcast_to(taps_ref[...], (144, reach)), 17, 1, stride=1, stride_axis=0
    ).astype(jnp.bfloat16)
    wide = lax.broadcasted_iota(jnp.int32, (reach, 3 * depth), 1)
    tall = lax.broadcasted_iota(jnp.int32, (reach, 3 * depth), 0)
    place = lax.rem(wide, slot)
    head, foot = place - inner_slot, place - inner_slot - 2 * edge + rows
    time = jnp.where(place < inner_slot, place + edge, jnp.where(head < edge, head, foot))
    used = (place < inner) | ((head >= 0) & (head < 2 * edge))
    hit = (tall == (wide // slot) * rows + time) & used
    expand_ref[...] = dot(compact, jnp.where(hit, 1.0, 0.0).astype(jnp.bfloat16)).astype(
        jnp.bfloat16
    )

    src = src_ref[...]
    belongs = (src // tile) == me
    chan = src - me * tile
    first = jnp.min(jnp.where(belongs, chan, tile), axis=1, keepdims=True)
    last = jnp.max(jnp.where(belongs, chan, -1), axis=1, keepdims=True)
    lane = lax.broadcasted_iota(jnp.int32, (n_blk, tile), 1)
    pickers = [
        jnp.where(lane == channel, 1.0, 0.0).astype(jnp.bfloat16) for channel in (first, last)
    ]
    row = src_ref[pl.ds(me, 1), :]
    column = turned(row)
    same = (row // tile) == (column // tile)
    later = jnp.max(jnp.where(same & (row < column), 1.0, 0.0), axis=1, keepdims=True)
    owner = lax.broadcasted_iota(jnp.int32, (n_src, n_blk), 1) == (column // tile)
    selectors = [
        jnp.where(owner & (later == float(which)), 1.0, 0.0).astype(jnp.bfloat16)
        for which in range(2)
    ]

    lax.fori_loop(1, n_blk, wait_block, 0)

    groups = n_blk // period
    for group in range(groups):
        low, high = max(group - 1, 0), min(group + 2, groups)
        skip = (low - group + 1) * depth
        held = recv_ref[low * period : high * period].reshape((high - low) * depth, tile)
        white_ref[group * 144 : (group + 1) * 144, :] = dot(
            expand_ref[:, skip : skip + (high - low) * depth], held
        ).astype(jnp.bfloat16)

    source_time = white_ref[LAGS // 2 : LAGS // 2 + span, :]
    for which in range(2):
        offer_ref[:, which, :] = dot(pickers[which], source_time, ((1,), (1,)))

    def source_copy(peer, place):
        return pltpu.make_async_remote_copy(
            offer_ref.at[peer], taken_ref.at[place],
            src_send.at[peer], src_recv.at[place], device_id={"blk": peer},
        )

    def send_source(step, carry):
        source_copy(lax.rem(me + step, n_blk), me).start()
        return carry

    def wait_source(step, carry):
        peer = lax.rem(me + step, n_blk)
        copy = source_copy(peer, peer)
        copy.wait_send()
        copy.wait_recv()
        return carry

    def window_copy(peer, place):
        return pltpu.make_async_remote_copy(
            white_ref.at[pl.ds(pl.multiple_of(peer * share, share), window)],
            got_ref.at[place, pl.ds(0, window)],
            win_send.at[peer], win_recv.at[place], device_id={"pair": peer},
        )

    def pick_copy(peer, place):
        return pltpu.make_async_remote_copy(
            pick_ref, got_ref.at[place, pl.ds(window, n_src)],
            pick_send.at[peer], pick_recv.at[place], device_id={"pair": peer},
        )

    pair_peers = [lax.rem(seg + step, n_pair) for step in range(1, n_pair)]
    pair_peers = pair_peers[1:] + pair_peers[:1]
    lax.fori_loop(1, n_blk, send_source, 0)
    for peer in pair_peers:
        window_copy(peer, seg).start()
    taken_ref[me] = offer_ref[me]
    got_ref[seg, 0:window] = white_ref[pl.ds(pl.multiple_of(seg * share, share), window), :]
    lax.fori_loop(1, n_blk, wait_source, 0)
    picked = jnp.zeros((n_src, span), jnp.float32)
    for which in range(2):
        picked += dot(selectors[which], taken_ref[:, which, :].astype(jnp.bfloat16))
    pick_ref[...] = picked.astype(jnp.bfloat16)
    for peer in pair_peers:
        pick_copy(peer, seg).start()
    got_ref[seg, window : window + n_src] = picked.astype(jnp.bfloat16)
    for peer in pair_peers:
        for copy in (window_copy(peer, peer), pick_copy(peer, peer)):
            copy.wait_send()
            copy.wait_recv()
    out_ref[...] = got_ref[...]


def correlate_kernel(span, n_src, got_ref, low_ref, high_ref, out_ref, lhs_ref, rhs_ref, src_ref, mask_ref):
    step = pl.program_id(0)
    segments, _, tile = got_ref.shape
    groups = out_ref.shape[0]
    reach = span + LAG_GROUP
    window = groups * LAG_GROUP + span

    @pl.when(step == 0)
    def _():
        gap = jnp.zeros((n_src, LAG_GROUP), jnp.float32)
        pieces = []
        for seg in range(segments):
            pieces += [got_ref[seg, window : window + n_src, :].astype(jnp.float32), gap]
            for group in range(groups):
                rhs_ref[seg * reach : (seg + 1) * reach, group * tile : (group + 1) * tile] = got_ref[
                    seg, group * LAG_GROUP : group * LAG_GROUP + reach, :
                ]
        src_ref[...] = jnp.concatenate(pieces, axis=1)
        low, high = turned(low_ref[...]), turned(high_ref[...])
        position = lax.broadcasted_iota(jnp.int32, (n_src, tile), 1)
        inside = (position >= low) & (position < high)
        scale = 1.0 / math.sqrt(span * segments)
        mask_ref[...] = jnp.where(inside, jnp.float32(scale), jnp.float32(0.0))

    base = src_ref[...]
    for lag in range(STEP_LAGS):
        rolled = pltpu.roll(base, lag, 1) if lag else base
        lhs_ref[lag * n_src : (lag + 1) * n_src, :] = rolled.astype(jnp.bfloat16)
    src_ref[...] = pltpu.roll(base, STEP_LAGS, 1)
    mask = mask_ref[...]
    for group in range(0, groups, 2):
        product = dot(lhs_ref[...], rhs_ref[:, group * tile : (group + 2) * tile])
        for half in range(2):
            piece = product[:, half * tile : (half + 1) * tile].reshape(STEP_LAGS, n_src, tile)
            out_ref[group + half] = piece * mask[None]


def body(raw_strain, aa_taps, white_taps, src_channels, recv_lo, recv_hi):
    raw_len = raw_strain.shape[1]
    short_len = raw_len // DECIM
    channels = raw_strain.shape[2]
    n_blocks = lax.axis_size("blk")
    n_pairs = lax.axis_size("pair")
    tile = channels // n_blocks
    seg_len = short_len * n_blocks
    span = seg_len - LAGS
    n_src = src_channels.shape[1]
    n_tiles = src_channels.shape[0]
    share = LAGS // n_pairs

    edge = KA // 2 // DECIM
    slot = rounded(short_len - 2 * edge, 16) + 16
    aa_width = rounded(DECIM * (slot + 3 * edge) + KA + KA // 2, BLOCK)
    depth = 144 // short_len * slot
    dma = pltpu.SemaphoreType.DMA
    vmem = pl.BlockSpec(memory_space=pltpu.VMEM)
    got = pl.pallas_call(
        lambda *refs: exchange_kernel(n_blocks, n_pairs, short_len, span, *refs),
        in_specs=[pl.BlockSpec(memory_space=pl.ANY)] + [vmem] * 3,
        out_specs=vmem,
        out_shape=jax.ShapeDtypeStruct((n_pairs, share + span + n_src, tile), jnp.bfloat16),
        scratch_shapes=[
            pltpu.VMEM((raw_len, channels), raw_strain.dtype),
            pltpu.VMEM((1, aa_width), jnp.float32),
            pltpu.VMEM((1, 4 * BLOCK), jnp.float32),
            pltpu.VMEM((2 * edge, channels), jnp.float32),
            *[pltpu.VMEM((edge, channels), jnp.float32)] * 4,
            *[pltpu.VMEM((n_blocks, slot, tile), jnp.bfloat16)] * 2,
            pltpu.VMEM((seg_len, tile), jnp.bfloat16),
            *[pltpu.VMEM((n_tiles, 2, span), jnp.float32)] * 2,
            pltpu.VMEM((n_src, span), jnp.bfloat16),
            pltpu.VMEM((n_pairs, share + span + n_src, tile), jnp.bfloat16),
            pltpu.VMEM((144, 3 * depth), jnp.bfloat16),
            dma((2,)), dma((2,)),
            *[dma((2, n_blocks))] * 2,
            *[dma((n_blocks,))] * 2,
            *[dma((n_pairs,))] * 4,
            dma((n_blocks // 8,)),
        ],
        compiler_params=pltpu.CompilerParams(collective_id=0, has_side_effects=True),
        name="exchange",
    )(raw_strain[0], aa_taps, white_taps, src_channels)

    groups = share // LAG_GROUP
    reach = n_pairs * (span + LAG_GROUP)
    whole = lambda *shape: pl.BlockSpec(shape, lambda i: (0,) * len(shape))
    xcorr = pl.pallas_call(
        lambda *refs: correlate_kernel(span, n_src, *refs),
        grid=(LAG_GROUP // STEP_LAGS,),
        in_specs=[whole(*got.shape), whole(1, n_src), whole(1, n_src)],
        out_specs=pl.BlockSpec((groups, STEP_LAGS, n_src, tile), lambda i: (0, i, 0, 0)),
        out_shape=jax.ShapeDtypeStruct((groups, LAG_GROUP, n_src, tile), jnp.float32),
        scratch_shapes=[
            pltpu.VMEM((STEP_LAGS * n_src, reach), jnp.bfloat16),
            pltpu.VMEM((reach, groups * tile), jnp.bfloat16),
            pltpu.VMEM((n_src, reach), jnp.float32),
            pltpu.VMEM((n_src, tile), jnp.float32),
        ],
        name="correlate",
    )(got, recv_lo, recv_hi)
    return xcorr.reshape(1, share, n_src, tile)


def solution(mesh):
    placed = (P("pair", "blk", None), P(), P(), P(), P("blk", None), P("blk", None))
    return jax.shard_map(
        body, mesh=mesh, in_specs=placed, out_specs=P("blk", "pair", None, None), check_vma=False
    )
```
